512 devices in a mesh: row: 16 (over z), col: 32 (over x, y, core).
Axes of the slice: x: 4, y: 4, z: 16, core: 2. Of those that a mesh axis runs over, the one named last changes fastest.
Arguments:
- children: float32 [2, 4096, 16384], P(None, 'row', 'col'), may hold values from -1 to 6, as said below
- block_maps: int32 [2, 64], replicated, may hold values from 0 to 63, each once within a row
Outputs:
- panel_rows: float32 [512, 16384], P(None, 'col')
- trailing: float32 [2, 4096, 16384], P(None, 'row', 'col')
The draws below stay inside these ranges and needn't reach their ends.
Inputs may be any that keep to these rules, and one draw needn't show every extreme that they name: Each row of block_maps names every parent column block once. `children`: each child's block is upper triangular in its own column order: entry (i, j) is zero where j < i.
All inputs are finite; a program needn't handle non-finite values.
Results may differ from the reference program's by a relative error of at most 0.000078.
Values sent between devices are 32-bit elements; how exact they have to be, the bound alone decides.
A program may use at most 64 MiB of HBM per device.

```python
import jax
import jax.numpy as jnp
from jax import lax

PANEL = 256
CROWS = 4096
NBLK = 64
NP = 16384


def draw_children(key, part):
    key_off, key_diag = jax.random.split(key, 2)
    row_index = jnp.arange(CROWS, dtype=jnp.int32)[None, :, None]
    col_index = jnp.arange(NP, dtype=jnp.int32)[None, None, :]
    offdiag = jnp.clip(0.15 * jax.random.normal(key_off, (2, CROWS, NP), jnp.float32), -0.9, 0.9)
    diagonal = jax.random.uniform(key_diag, (2, CROWS, 1), jnp.float32, 3.0, 6.0)
    upper = jnp.where(col_index > row_index, offdiag, 0.0)
    return jnp.where(col_index == row_index, diagonal, upper).astype(jnp.float32)


def setup_inputs(seed: int = 0) -> dict:
    arg_keys = jax.random.split(jax.random.key(seed), 3)
    return {
        "children": draw_children(jax.random.fold_in(arg_keys[2], 71), 0),
        "block_maps": jax.vmap(lambda own: jax.random.permutation(own, NBLK))(jax.random.split(arg_keys[1], 2)).reshape((2, NBLK)).astype(jnp.int32),
    }


def crossed(left_matrix, right_matrix):
    return jnp.dot(left_matrix.T.astype(jnp.float32), right_matrix.astype(jnp.float32), precision=lax.Precision.HIGHEST, preferred_element_type=jnp.float32)

def applied(left_matrix, right_matrix):
    return jnp.dot(left_matrix.astype(jnp.float32), right_matrix.astype(jnp.float32), precision=lax.Precision.HIGHEST, preferred_element_type=jnp.float32)

def orthonormal(panel_cols):
    factor = jnp.linalg.cholesky(crossed(panel_cols, panel_cols))
    return lax.linalg.triangular_solve(factor, panel_cols, left_side=False, lower=True, transpose_a=True)

def placed(child_rows, mapping):
    block_count = NP // PANEL
    inverse = jnp.zeros((block_count,), jnp.int32).at[mapping].set(jnp.arange(block_count, dtype=jnp.int32))
    blocks = child_rows.reshape(CROWS, block_count, PANEL)
    return jnp.take(blocks, inverse, axis=1).reshape(CROWS, NP)

def reference(children, block_maps):
    front = jnp.concatenate([placed(children[0], block_maps[0]), placed(children[1], block_maps[1])], axis=0)
    basis_one = orthonormal(front[:, :PANEL])
    rows_one = crossed(basis_one, front)
    front = front - applied(basis_one, rows_one)
    basis_two = orthonormal(front[:, PANEL:2 * PANEL])
    rows_two = crossed(basis_two, front)
    front = front - applied(basis_two, rows_two)
    return (jnp.concatenate([rows_one, rows_two], axis=0), front.reshape(2, CROWS, NP))
```

```python
import functools

import jax
import jax.numpy as jnp
from jax import lax
from jax.experimental import pallas as pl
from jax.experimental.pallas import tpu as pltpu
from jax.sharding import PartitionSpec as P

PANEL = 256
WIDE = 2 * PANEL
F32 = jnp.float32
BF16 = jnp.bfloat16
MESH = pl.DeviceIdType.MESH
VMEM = pl.BlockSpec(memory_space=pltpu.VMEM)
SMEM = pl.BlockSpec(memory_space=pltpu.SMEM)


def split(x):
    high = x.astype(BF16)
    low = (x - high.astype(F32)).astype(BF16)
    return high, low


def product(a, b, dims=((1,), (0,))):
    def one(x, y):
        return lax.dot_general(x, y, (dims, ((), ())), preferred_element_type=F32)

    return one(a[0], b[0]) + (one(a[0], b[1]) + one(a[1], b[0]))


def exchange_kernel(ncol, rows, inv_ref, kids_ref, front_ref, panel_ref, got, out, sems):
    me = lax.axis_index("col")
    barrier = pltpu.get_barrier_semaphore()

    @pl.loop(1, ncol)
    def _(d):
        pl.semaphore_signal(barrier, inc=1, device_id={"col": lax.rem(me + d, ncol)}, device_id_type=MESH)

    pl.semaphore_wait(barrier, ncol - 1)

    def send(src, dst, phase, to):
        pltpu.make_async_remote_copy(
            src_ref=src,
            dst_ref=dst,
            send_sem=sems.at[2 * phase],
            recv_sem=sems.at[2 * phase + 1],
            device_id={"col": to},
            device_id_type=MESH,
        ).start()

    def drain(ref, which):
        pltpu.make_async_copy(ref, ref, sems.at[which]).wait()

    def slab(owner):
        return pl.ds(pl.multiple_of(owner * rows, rows), rows)

    @pl.loop(1, ncol)
    def _(d):
        to = lax.rem(me + d, ncol)
        send(kids_ref.at[:, slab(to), :], got.at[me], 0, to)

    got[me] = kids_ref[:, slab(me), :]
    many = out.at[pl.ds(0, ncol - 1)]
    drain(got.at[pl.ds(0, ncol - 1)], 1)

    def place(to):
        for child in range(2):
            for half in range(2):
                block = inv_ref[child, 2 * to + half]
                pair = got[block // 2, child]
                low = jnp.broadcast_to(lax.rem(block, 2), (rows, PANEL)) == 0
                out[to, child, :, half * PANEL : (half + 1) * PANEL] = jnp.where(
                    low, pair[:, :PANEL], pair[:, PANEL:]
                )

    place(0)

    @pl.loop(1, ncol)
    def _(d):
        to = lax.rem(me + d, ncol)
        send(out.at[0], panel_ref.at[:, slab(me), :], 1, to)

    panel_ref[:, slab(me), :] = out[0]

    @pl.loop(1, ncol)
    def _(to):
        place(to)

    @pl.loop(1, ncol)
    def _(d):
        to = lax.rem(me + d, ncol)
        send(out.at[to], front_ref.at[:, slab(me), :], 2, to)

    front_ref[:, slab(me), :] = out[me]
    drain(many, 0)
    drain(many, 2)
    drain(many, 3)
    drain(many, 4)
    drain(many, 5)


def exchange(children, inverse, ncol):
    rows_dev = children.shape[1]
    rows = rows_dev // ncol
    piece = jax.ShapeDtypeStruct((2, rows_dev, WIDE), F32)
    return pl.pallas_call(
        functools.partial(exchange_kernel, ncol, rows),
        out_shape=(piece, piece),
        in_specs=[SMEM, VMEM],
        out_specs=(VMEM, VMEM),
        scratch_shapes=[
            pltpu.VMEM((ncol, 2, rows, WIDE), F32),
            pltpu.VMEM((ncol, 2, rows, WIDE), F32),
            pltpu.SemaphoreType.DMA((6,)),
        ],
        compiler_params=pltpu.CompilerParams(
            collective_id=0, has_side_effects=True, vmem_limit_bytes=32 << 20
        ),
        name="exchange",
    )(inverse, children)


def eliminate(gram, linv, base, k):
    top = pl.multiple_of(8 * k, 8)
    rows = gram[pl.ds(top, 8), :]
    inv_rows = linv[pl.ds(top, 8), :]
    turned = pltpu.roll(rows, lax.rem(128 - 8 * k, 128), axis=1)
    cols = [jnp.broadcast_to(turned[:, j : j + 1], (8, 128)) for j in range(8)]
    sub = lax.broadcasted_iota(jnp.int32, (8, 128), 0)
    for p in range(8):
        pivot = jnp.broadcast_to(cols[p][p : p + 1, :], (8, 128))
        recip = 1.0 / pivot
        root = lax.rsqrt(pivot)
        mult = jnp.where(sub > p, cols[p] * recip, 0.0)
        for j in range(p + 1, 8):
            cols[j] = cols[j] - mult * jnp.broadcast_to(cols[p][j : j + 1, :], (8, 128))
        row = jnp.broadcast_to(rows[p : p + 1, :], (8, 128))
        inv_row = jnp.broadcast_to(inv_rows[p : p + 1, :], (8, 128))
        scale = jnp.where(sub == p, root, 1.0)
        rows = (rows - mult * row) * scale
        inv_rows = (inv_rows - mult * inv_row) * scale
    gram[pl.ds(top, 8), :] = rows
    linv[pl.ds(top, 8), :] = inv_rows
    both = jnp.concatenate([rows, inv_rows], axis=1)
    update = lax.dot_general(
        rows, both, (((0,), (0,)), ((), ())), precision=lax.Precision.HIGHEST, preferred_element_type=F32
    )
    below = lax.broadcasted_iota(jnp.int32, (128, 128), 0) >= top + 8
    gram[...] = gram[...] - jnp.where(below, update[:, :128], 0.0)
    linv[...] = linv[...] - jnp.where(below, update[:, 128:], 0.0)


def reduce_kernel(
    nrow, ncol, front_ref, panel_ref, s_ref, linv_ref,
    local, gram, tiles, part, up, down, diag, dinv, sems, ring
):
    me = lax.axis_index("col")
    mz = lax.axis_index("row")
    strip = WIDE // ncol
    chunk = WIDE // nrow
    ntile = strip // 8 * (WIDE // 128)
    barrier = pltpu.get_barrier_semaphore()

    @pl.loop(1, ncol)
    def _(d):
        pl.semaphore_signal(barrier, inc=1, device_id={"col": lax.rem(me + d, ncol)}, device_id_type=MESH)

    @pl.loop(1, nrow)
    def _(d):
        pl.semaphore_signal(barrier, inc=1, device_id={"row": lax.rem(mz + d, nrow)}, device_id_type=MESH)

    pan = panel_ref[...].reshape(-1, WIDE)
    pan_t = split(pan.T)
    local[...] = product(pan_t, split(pan))
    pl.semaphore_wait(barrier, ncol + nrow - 2)

    def send(src, dst, sem, phase, to):
        pltpu.make_async_remote_copy(
            src_ref=src,
            dst_ref=dst,
            send_sem=sem.at[2 * phase],
            recv_sem=sem.at[2 * phase + 1],
            device_id=to,
            device_id_type=MESH,
        ).start()

    def drain(ref, sem, which):
        pltpu.make_async_copy(ref, ref, sem.at[which]).wait()

    def tile_at(z):
        t = lax.rem(z, ntile)
        top = me * strip + (t // 4) * 8
        return pl.ds(pl.multiple_of(top, 8), 8), pl.ds(pl.multiple_of(lax.rem(t, 4) * 128, 128), 128)

    def my_strip():
        return pl.ds(pl.multiple_of(me * strip, 8), strip)

    @pl.loop(1, nrow)
    def _(d):
        to = lax.rem(mz + d, nrow)
        r, c = tile_at(to)
        send(local.at[r, c], tiles.at[mz], sems, 0, {"row": to})

    r, c = tile_at(mz)
    tiles[mz] = local[r, c]
    drain(tiles.at[pl.ds(0, nrow - 1)], sems, 1)
    total = tiles[0]
    for z in range(1, nrow):
        total = total + tiles[z]
    gram[r, c] = total
    offsets = [d for d in range(-(ntile // 2), ntile // 2) if d]
    for d in offsets:
        send(gram.at[r, c], gram.at[r, c], sems, 1, {"row": lax.rem(mz + d + nrow, nrow)})
    fr = split(front_ref[...].reshape(-1, WIDE))
    whole = product(pan_t, fr)
    part[...] = whole.reshape(nrow, chunk, WIDE)
    drain(tiles.at[pl.ds(0, ntile - 1)], sems, 3)

    @pl.loop(1, ncol)
    def _(d):
        to = lax.rem(me + d, ncol)
        send(gram.at[my_strip(), :], gram.at[my_strip(), :], sems, 2, {"col": to})

    half = nrow // 2
    after = {"row": lax.rem(mz + 1, nrow)}
    before = {"row": lax.rem(mz + nrow - 1, nrow)}

    def at(offset):
        return lax.rem(mz + offset + 2 * nrow, nrow)

    def copy(src, dst, index, to):
        return pltpu.make_async_remote_copy(
            src_ref=src, dst_ref=dst, send_sem=ring.at[0, index], recv_sem=ring.at[1, index],
            device_id=to, device_id_type=MESH,
        )

    def scatter_down(s):
        src = part.at[at(-half)] if s == 0 else down.at[s - 1]
        return copy(src, down.at[s], s, before)

    def scatter_up(s):
        src = part.at[at(half - 1)] if s == 0 else up.at[s - 1]
        return copy(src, up.at[s], half + s, after)

    def gather_up(s):
        here = s_ref.at[at(-s)]
        return copy(here, here, 2 * half + s, after)

    def gather_down(s):
        here = s_ref.at[at(s)]
        return copy(here, here, 3 * half + s, before)

    def ring_step(s):
        if s == 0:
            scatter_down(0).start()
            scatter_up(0).start()
        elif s < half:
            scatter_down(s - 1).wait()
            down[s - 1] = down[s - 1] + part[at(s - half)]
            scatter_down(s).start()
            scatter_up(s - 1).wait()
            if s < half - 1:
                up[s - 1] = up[s - 1] + part[at(half - 1 - s)]
                scatter_up(s).start()
        elif s == half:
            scatter_down(half - 1).wait()
            s_ref[mz] = part[mz] + up[half - 2] + down[half - 1]
            gather_up(0).start()
            gather_down(0).start()
        else:
            q = s - half
            gather_up(q - 1).wait()
            if q < half:
                gather_up(q).start()
            if q < half:
                gather_down(q - 1).wait()
                if q < half - 1:
                    gather_down(q).start()

    ring_step(0)
    drain(gram.at[pl.ds(0, WIDE - strip), :], sems, 5)
    drain(tiles.at[pl.ds(0, ntile - 1)], sems, 2)
    drain(gram.at[pl.ds(0, WIDE - strip), :], sems, 4)
    linv_ref[...] = jnp.zeros((WIDE, WIDE), F32)
    row_id = lax.broadcasted_iota(jnp.int32, (128, 128), 0)
    col_id = lax.broadcasted_iota(jnp.int32, (128, 128), 1)
    eye = jnp.where(row_id == col_id, 1.0, 0.0)
    step = 1
    for ob in range(WIDE // 128):
        lo, hi = 128 * ob, 128 * (ob + 1)
        diag[...] = gram[lo:hi, lo:hi]
        dinv[...] = eye
        for quarter in range(4):

            @pl.loop(0, 4)
            def _(i):
                eliminate(diag, dinv, ob, 4 * quarter + i)

            if step <= 2 * half:
                ring_step(step)
                step += 1
        inv = split(jnp.where(row_id >= col_id, dinv[...], 0.0))
        linv_ref[lo:hi, lo:hi] = jnp.where(row_id >= col_id, dinv[...], 0.0)
        if ob:
            linv_ref[lo:hi, :lo] = product(inv, split(linv_ref[lo:hi, :lo]))
        if hi < WIDE:
            right = product(inv, split(gram[lo:hi, hi:]))
            right_t = split(right.T)
            gram[hi:, hi:] = gram[hi:, hi:] - product(right_t, split(right))
            linv_ref[hi:, :hi] = linv_ref[hi:, :hi] - product(right_t, split(linv_ref[lo:hi, :hi]))
    while step <= 2 * half:
        ring_step(step)
        step += 1
    drain(tiles.at[pl.ds(0, nrow - 1)], sems, 0)


def reduced(front, panel, nrow, ncol):
    chunk = WIDE // nrow
    half = nrow // 2
    return pl.pallas_call(
        functools.partial(reduce_kernel, nrow, ncol),
        out_shape=(
            jax.ShapeDtypeStruct((nrow, chunk, WIDE), F32),
            jax.ShapeDtypeStruct((WIDE, WIDE), F32),
        ),
        in_specs=[VMEM, VMEM],
        out_specs=(VMEM, VMEM),
        scratch_shapes=[
            pltpu.VMEM((WIDE, WIDE), F32),
            pltpu.VMEM((WIDE, WIDE), F32),
            pltpu.VMEM((nrow, 8, 128), F32),
            pltpu.VMEM((nrow, chunk, WIDE), F32),
            pltpu.VMEM((half - 1, chunk, WIDE), F32),
            pltpu.VMEM((half, chunk, WIDE), F32),
            pltpu.VMEM((128, 128), F32),
            pltpu.VMEM((128, 128), F32),
            pltpu.SemaphoreType.DMA((6,)),
            pltpu.SemaphoreType.DMA((2, 4 * half)),
        ],
        compiler_params=pltpu.CompilerParams(
            collective_id=1, has_side_effects=True, vmem_limit_bytes=48 << 20
        ),
        name="reduce_and_factor",
    )(front, panel)


def finish_kernel(front_ref, panel_ref, s_ref, linv_ref, rows_ref, trail_ref):
    inv = split(linv_ref[...])
    upper = product(inv, split(s_ref[...].reshape(WIDE, WIDE)))
    rows_ref[...] = upper
    back = product(split(linv_ref[...].T), split(upper))
    pan = panel_ref[...].reshape(-1, WIDE)
    trail_ref[...] = front_ref[...] - product(split(pan), split(back)).reshape(front_ref.shape)


def finish(front, panel, s, linv):
    return pl.pallas_call(
        finish_kernel,
        out_shape=(
            jax.ShapeDtypeStruct((WIDE, WIDE), F32),
            jax.ShapeDtypeStruct(front.shape, F32),
        ),
        in_specs=[VMEM] * 4,
        out_specs=(VMEM, VMEM),
        compiler_params=pltpu.CompilerParams(vmem_limit_bytes=48 << 20),
        name="finish",
    )(front, panel, s, linv)


def inverted(maps):
    count = maps.shape[1]
    ids = lax.broadcasted_iota(jnp.int32, (2, count, count), 1)
    hit = maps[:, :, None] == lax.broadcasted_iota(jnp.int32, (2, count, count), 2)
    return jnp.sum(jnp.where(hit, ids, 0), axis=1)


def per_device(children, block_maps):
    ncol = lax.axis_size("col")
    nrow = lax.axis_size("row")
    front, panel = exchange(children, inverted(block_maps), ncol)
    s, linv = reduced(front, panel, nrow, ncol)
    return finish(front, panel, s, linv)


def solution(mesh):
    placed = (P(None, "row", "col"), P())
    return jax.shard_map(
        per_device,
        mesh=mesh,
        in_specs=placed,
        out_specs=(P(None, "col"), P(None, "row", "col")),
        check_vma=False,
    )
```

```python
import functools

import jax
import jax.numpy as jnp
from jax import lax
from jax.experimental import pallas as pl
from jax.experimental.pallas import tpu as pltpu
from jax.sharding import PartitionSpec as P

PANEL = 256
WIDE = 2 * PANEL
F32 = jnp.float32
BF16 = jnp.bfloat16
MESH = pl.DeviceIdType.MESH
VMEM = pl.BlockSpec(memory_space=pltpu.VMEM)
SMEM = pl.BlockSpec(memory_space=pltpu.SMEM)


def split(x):
    high = x.astype(BF16)
    low = (x - high.astype(F32)).astype(BF16)
    return high, low


def product(a, b, dims=((1,), (0,))):
    def one(x, y):
        return lax.dot_general(x, y, (dims, ((), ())), preferred_element_type=F32)

    return one(a[0], b[0]) + (one(a[0], b[1]) + one(a[1], b[0]))


def eliminate(gram, linv, base, k):
    top = pl.multiple_of(8 * k, 8)
    rows = gram[pl.ds(top, 8), :]
    inv_rows = linv[pl.ds(top, 8), :]
    turned = pltpu.roll(rows, lax.rem(128 - 8 * k, 128), axis=1)
    cols = [jnp.broadcast_to(turned[:, j : j + 1], (8, 128)) for j in range(8)]
    sub = lax.broadcasted_iota(jnp.int32, (8, 128), 0)
    for p in range(8):
        pivot = jnp.broadcast_to(cols[p][p : p + 1, :], (8, 128))
        recip = 1.0 / pivot
        root = lax.rsqrt(pivot)
        mult = jnp.where(sub > p, cols[p] * recip, 0.0)
        for j in range(p + 1, 8):
            cols[j] = cols[j] - mult * jnp.broadcast_to(cols[p][j : j + 1, :], (8, 128))
        row = jnp.broadcast_to(rows[p : p + 1, :], (8, 128))
        inv_row = jnp.broadcast_to(inv_rows[p : p + 1, :], (8, 128))
        scale = jnp.where(sub == p, root, 1.0)
        rows = (rows - mult * row) * scale
        inv_rows = (inv_rows - mult * inv_row) * scale
    gram[pl.ds(top, 8), :] = rows
    linv[pl.ds(top, 8), :] = inv_rows
    both = jnp.concatenate([rows, inv_rows], axis=1)
    update = lax.dot_general(
        rows, both, (((0,), (0,)), ((), ())), precision=lax.Precision.HIGHEST, preferred_element_type=F32
    )
    below = lax.broadcasted_iota(jnp.int32, (128, 128), 0) >= top + 8
    gram[...] = gram[...] - jnp.where(below, update[:, :128], 0.0)
    linv[...] = linv[...] - jnp.where(below, update[:, 128:], 0.0)


def merge_kernel(
    nrow, ncol, inv_ref, kids_ref, front_ref, panel_ref, s_ref, linv_ref,
    got, out, local, gram, tiles, part, up, down, diag, dinv, sems, ring
):
    me = lax.axis_index("col")
    mz = lax.axis_index("row")
    rows = kids_ref.shape[1] // ncol
    strip = WIDE // ncol
    chunk = WIDE // nrow
    ntile = strip // 8 * (WIDE // 128)
    core = lax.rem(me, 2)
    twin = me + 1 - 2 * core
    chips = ncol // 2
    barrier = pltpu.get_barrier_semaphore()

    @pl.loop(1, ncol)
    def _(d):
        pl.semaphore_signal(barrier, inc=1, device_id={"col": lax.rem(me + d, ncol)}, device_id_type=MESH)

    @pl.loop(1, nrow)
    def _(d):
        pl.semaphore_signal(barrier, inc=1, device_id={"row": lax.rem(mz + d, nrow)}, device_id_type=MESH)

    pl.semaphore_wait(barrier, ncol + nrow - 2)

    def send(src, dst, phase, to):
        pltpu.make_async_remote_copy(
            src_ref=src,
            dst_ref=dst,
            send_sem=sems.at[2 * phase],
            recv_sem=sems.at[2 * phase + 1],
            device_id=to,
            device_id_type=MESH,
        ).start()

    def drain(ref, which):
        pltpu.make_async_copy(ref, ref, sems.at[which]).wait()

    def slab(owner):
        return pl.ds(pl.multiple_of(owner * rows, rows), rows)

    def strip_of(owner):
        return pl.ds(pl.multiple_of(owner * strip, strip), strip)

    @pl.loop(1, ncol)
    def _(d):
        to = lax.rem(me + d, ncol)
        send(kids_ref.at[:, slab(to), :], got.at[me], 0, {"col": to})

    got[me] = kids_ref[:, slab(me), :]
    drain(got.at[pl.ds(0, ncol - 1)], 1)

    def place(to):
        for child in range(2):
            for half in range(2):
                block = inv_ref[child, 2 * to + half]
                pair = got[block // 2, child]
                low = jnp.broadcast_to(lax.rem(block, 2), (rows, PANEL)) == 0
                out[to, child, :, half * PANEL : (half + 1) * PANEL] = jnp.where(
                    low, pair[:, :PANEL], pair[:, PANEL:]
                )

    place(0)

    @pl.loop(1, chips)
    def _(d):
        send(out.at[0], panel_ref.at[:, slab(me), :], 1, {"col": lax.rem(me + 2 * d, ncol)})

    panel_ref[:, slab(me), :] = out[0]

    @pl.loop(1, ncol)
    def _(to):
        place(to)

    @pl.loop(1, ncol)
    def _(d):
        to = lax.rem(me + d, ncol)
        send(out.at[to], front_ref.at[:, slab(me), :], 2, {"col": to})

    front_ref[:, slab(me), :] = out[me]
    drain(out.at[pl.ds(0, chips - 1)], 3)

    @pl.loop(0, chips)
    def _(i):
        here = panel_ref.at[:, slab(2 * i + core), :]
        send(here, here, 3, {"col": twin})

    drain(out.at[pl.ds(0, chips)], 7)

    pan = panel_ref[...].reshape(-1, WIDE)
    pan_t = split(pan.T)
    local[...] = product(pan_t, split(pan))

    def tile_at(z):
        t = lax.rem(z, ntile)
        top = me * strip + (t // 4) * 8
        return pl.ds(pl.multiple_of(top, 8), 8), pl.ds(pl.multiple_of(lax.rem(t, 4) * 128, 128), 128)

    @pl.loop(1, nrow)
    def _(d):
        to = lax.rem(mz + d, nrow)
        r, c = tile_at(to)
        send(local.at[r, c], tiles.at[mz], 4, {"row": to})

    r, c = tile_at(mz)
    tiles[mz] = local[r, c]
    drain(tiles.at[pl.ds(0, nrow - 1)], 9)
    total = tiles[0]
    for z in range(1, nrow):
        total = total + tiles[z]
    gram[r, c] = total
    for d in range(-(ntile // 2), ntile // 2):
        if d:
            send(gram.at[r, c], gram.at[r, c], 5, {"row": lax.rem(mz + d + nrow, nrow)})
    drain(tiles.at[pl.ds(0, ntile - 1)], 11)

    @pl.loop(1, chips)
    def _(d):
        here = gram.at[strip_of(me), :]
        send(here, here, 6, {"col": lax.rem(me + 2 * d, ncol)})

    drain(out.at[pl.ds(0, ncol - 1)], 5)
    fr = split(front_ref[...].reshape(-1, WIDE))
    part[...] = product(pan_t, fr).reshape(nrow, chunk, WIDE)

    half = nrow // 2
    after = {"row": lax.rem(mz + 1, nrow)}
    before = {"row": lax.rem(mz + nrow - 1, nrow)}

    def at(offset):
        return lax.rem(mz + offset + 2 * nrow, nrow)

    def copy(src, dst, index, to):
        return pltpu.make_async_remote_copy(
            src_ref=src, dst_ref=dst, send_sem=ring.at[0, index], recv_sem=ring.at[1, index],
            device_id=to, device_id_type=MESH,
        )

    def scatter_down(s):
        src = part.at[at(-half)] if s == 0 else down.at[s - 1]
        return copy(src, down.at[s], s, before)

    def scatter_up(s):
        src = part.at[at(half - 1)] if s == 0 else up.at[s - 1]
        return copy(src, up.at[s], half + s, after)

    def gather_up(s):
        here = s_ref.at[at(-s)]
        return copy(here, here, 2 * half + s, after)

    def gather_down(s):
        here = s_ref.at[at(s)]
        return copy(here, here, 3 * half + s, before)

    def ring_step(s):
        if s == 0:
            scatter_down(0).start()
            scatter_up(0).start()
        elif s < half:
            scatter_down(s - 1).wait()
            down[s - 1] = down[s - 1] + part[at(s - half)]
            scatter_down(s).start()
            scatter_up(s - 1).wait()
            if s < half - 1:
                up[s - 1] = up[s - 1] + part[at(half - 1 - s)]
                scatter_up(s).start()
        elif s == half:
            scatter_down(half - 1).wait()
            s_ref[mz] = part[mz] + up[half - 2] + down[half - 1]
            gather_up(0).start()
            gather_down(0).start()
        else:
            q = s - half
            gather_up(q - 1).wait()
            if q < half:
                gather_up(q).start()
            if q < half:
                gather_down(q - 1).wait()
                if q < half - 1:
                    gather_down(q).start()

    ring_step(0)
    drain(out.at[pl.ds(0, chips - 1)], 13)

    @pl.loop(0, chips)
    def _(i):
        here = gram.at[strip_of(2 * i + core), :]
        send(here, here, 7, {"col": twin})

    drain(out.at[pl.ds(0, chips)], 15)
    drain(out.at[pl.ds(0, chips)], 14)
    drain(out.at[pl.ds(0, chips - 1)], 12)
    drain(tiles.at[pl.ds(0, ntile - 1)], 10)
    linv_ref[...] = jnp.zeros((WIDE, WIDE), F32)
    row_id = lax.broadcasted_iota(jnp.int32, (128, 128), 0)
    col_id = lax.broadcasted_iota(jnp.int32, (128, 128), 1)
    eye = jnp.where(row_id == col_id, 1.0, 0.0)
    step = 1
    for ob in range(WIDE // 128):
        lo, hi = 128 * ob, 128 * (ob + 1)
        diag[...] = gram[lo:hi, lo:hi]
        dinv[...] = eye
        for quarter in range(4):

            @pl.loop(0, 4)
            def _(i):
                eliminate(diag, dinv, ob, 4 * quarter + i)

            if step <= 2 * half:
                ring_step(step)
                step += 1
        inv = split(jnp.where(row_id >= col_id, dinv[...], 0.0))
        linv_ref[lo:hi, lo:hi] = jnp.where(row_id >= col_id, dinv[...], 0.0)
        if ob:
            linv_ref[lo:hi, :lo] = product(inv, split(linv_ref[lo:hi, :lo]))
        if hi < WIDE:
            right = product(inv, split(gram[lo:hi, hi:]))
            right_t = split(right.T)
            gram[hi:, hi:] = gram[hi:, hi:] - product(right_t, split(right))
            linv_ref[hi:, :hi] = linv_ref[hi:, :hi] - product(right_t, split(linv_ref[lo:hi, :hi]))
    while step <= 2 * half:
        ring_step(step)
        step += 1
    drain(tiles.at[pl.ds(0, nrow - 1)], 8)
    drain(out.at[pl.ds(0, chips)], 6)
    drain(out.at[pl.ds(0, ncol - 1)], 4)
    drain(out.at[pl.ds(0, chips - 1)], 2)
    drain(out.at[pl.ds(0, ncol - 1)], 0)


def merged(children, inverse, nrow, ncol):
    rows_dev = children.shape[1]
    chunk = WIDE // nrow
    half = nrow // 2
    piece = jax.ShapeDtypeStruct((2, rows_dev, WIDE), F32)
    slices = pltpu.VMEM((ncol, 2, rows_dev // ncol, WIDE), F32)
    return pl.pallas_call(
        functools.partial(merge_kernel, nrow, ncol),
        out_shape=(
            piece,
            piece,
            jax.ShapeDtypeStruct((nrow, chunk, WIDE), F32),
            jax.ShapeDtypeStruct((WIDE, WIDE), F32),
        ),
        in_specs=[SMEM, VMEM],
        out_specs=(VMEM, VMEM, VMEM, VMEM),
        scratch_shapes=[
            slices,
            slices,
            pltpu.VMEM((WIDE, WIDE), F32),
            pltpu.VMEM((WIDE, WIDE), F32),
            pltpu.VMEM((nrow, 8, 128), F32),
            pltpu.VMEM((nrow, chunk, WIDE), F32),
            pltpu.VMEM((half - 1, chunk, WIDE), F32),
            pltpu.VMEM((half, chunk, WIDE), F32),
            pltpu.VMEM((128, 128), F32),
            pltpu.VMEM((128, 128), F32),
            pltpu.SemaphoreType.DMA((16,)),
            pltpu.SemaphoreType.DMA((2, 4 * half)),
        ],
        compiler_params=pltpu.CompilerParams(
            collective_id=0, has_side_effects=True, vmem_limit_bytes=48 << 20
        ),
        name="merge",
    )(inverse, children)


def finish_kernel(front_ref, panel_ref, s_ref, linv_ref, rows_ref, trail_ref):
    inv = split(linv_ref[...])
    upper = product(inv, split(s_ref[...].reshape(WIDE, WIDE)))
    rows_ref[...] = upper
    back = product(split(linv_ref[...].T), split(upper))
    pan = panel_ref[...].reshape(-1, WIDE)
    trail_ref[...] = front_ref[...] - product(split(pan), split(back)).reshape(front_ref.shape)


def finish(front, panel, s, linv):
    return pl.pallas_call(
        finish_kernel,
        out_shape=(
            jax.ShapeDtypeStruct((WIDE, WIDE), F32),
            jax.ShapeDtypeStruct(front.shape, F32),
        ),
        in_specs=[VMEM] * 4,
        out_specs=(VMEM, VMEM),
        compiler_params=pltpu.CompilerParams(vmem_limit_bytes=48 << 20),
        name="finish",
    )(front, panel, s, linv)


def inverted(maps):
    count = maps.shape[1]
    ids = lax.broadcasted_iota(jnp.int32, (2, count, count), 1)
    hit = maps[:, :, None] == lax.broadcasted_iota(jnp.int32, (2, count, count), 2)
    return jnp.sum(jnp.where(hit, ids, 0), axis=1)


def per_device(children, block_maps):
    ncol = lax.axis_size("col")
    nrow = lax.axis_size("row")
    front, panel, s, linv = merged(children, inverted(block_maps), nrow, ncol)
    return finish(front, panel, s, linv)


def solution(mesh):
    placed = (P(None, "row", "col"), P())
    return jax.shard_map(
        per_device,
        mesh=mesh,
        in_specs=placed,
        out_specs=(P(None, "col"), P(None, "row", "col")),
        check_vma=False,
    )
```

```python
import functools
import math

import jax
import jax.numpy as jnp
from jax import lax
from jax.experimental import pallas as pl
from jax.experimental.pallas import tpu as pltpu
from jax.sharding import PartitionSpec as P

PANEL = 256
WIDE = 2 * PANEL
F32 = jnp.float32
BF16 = jnp.bfloat16
MESH = pl.DeviceIdType.MESH
VMEM = pl.BlockSpec(memory_space=pltpu.VMEM)
SMEM = pl.BlockSpec(memory_space=pltpu.SMEM)


def split(x):
    high = x.astype(BF16)
    low = (x - high.astype(F32)).astype(BF16)
    return high, low


def product(a, b, dims=((1,), (0,))):
    def one(x, y):
        return lax.dot_general(x, y, (dims, ((), ())), preferred_element_type=F32)

    return one(a[0], b[0]) + (one(a[0], b[1]) + one(a[1], b[0]))


DEEP = 16


def eliminate(gram, linv, k):
    groups = DEEP // 8
    top = pl.multiple_of(DEEP * k, DEEP)
    rows = [gram[pl.ds(top + 8 * g, 8), :] for g in range(groups)]
    invs = [linv[pl.ds(top + 8 * g, 8), :] for g in range(groups)]
    cols = []
    for g in range(groups):
        turned = pltpu.roll(rows[g], lax.rem(128 - DEEP * k, 128), axis=1)
        cols.append([jnp.broadcast_to(turned[:, j : j + 1], (8, 128)) for j in range(DEEP)])
    sub = lax.broadcasted_iota(jnp.int32, (8, 128), 0)

    def spread(value, i):
        return jnp.broadcast_to(value[i : i + 1, :], (8, 128))

    for p in range(DEEP):
        home, i = divmod(p, 8)
        pivot = spread(cols[home][p], i)
        recip = 1.0 / pivot
        mult = {}
        for g in range(home, groups):
            mult[g] = cols[g][p] * recip
        mult[home] = jnp.where(sub > i, mult[home], 0.0)
        for j in range(p + 1, DEEP):
            across = spread(cols[j // 8][p], j % 8)
            for g in range(j // 8, groups):
                cols[g][j] = cols[g][j] - mult[g] * across
        row, inv = spread(rows[home], i), spread(invs[home], i)
        for g in range(home, groups):
            rows[g] = rows[g] - mult[g] * row
            invs[g] = invs[g] - mult[g] * inv
        scale = jnp.where(sub == i, lax.rsqrt(pivot), 1.0)
        rows[home] = rows[home] * scale
        invs[home] = invs[home] * scale
    both = jnp.concatenate([jnp.concatenate(rows, axis=0), jnp.concatenate(invs, axis=0)], axis=1)
    gram[pl.ds(top, DEEP), :] = both[:, :128]
    linv[pl.ds(top, DEEP), :] = both[:, 128:]
    high, low = split(both)
    left = jnp.concatenate([high[:, :128], low[:, :128], high[:, :128]], axis=0)
    update = lax.dot_general(
        left,
        jnp.concatenate([high, high, low], axis=0),
        (((0,), (0,)), ((), ())),
        preferred_element_type=F32,
    )
    below = lax.broadcasted_iota(jnp.int32, (128, 128), 0) >= top + DEEP
    gram[...] = gram[...] - jnp.where(below, update[:, :128], 0.0)
    linv[...] = linv[...] - jnp.where(below, update[:, 128:], 0.0)


def orders(ncol):
    side = math.isqrt(ncol // 2)
    span = [(x, y, c) for x in range(side) for y in range(side) for c in range(2)]

    def far(o):
        return min(o[0], side - o[0]) + min(o[1], side - o[1])

    every = sorted(span[1:], key=lambda o: -far(o))
    return every, [o for o in every if o[2] == 0]


def merge_kernel(
    nrow, ncol, inv_ref, kids_ref, front_ref, panel_ref, s_ref, linv_ref,
    got, out, local, gram, tiles, part, pair_down, pair_up, sum_down, sum_up, diag, dinv, sems, ring
):
    me = lax.axis_index("col")
    mz = lax.axis_index("row")
    rows = kids_ref.shape[1] // ncol
    strip = WIDE // ncol
    chunk = WIDE // nrow
    ntile = strip // 8 * (WIDE // 128)
    core = lax.rem(me, 2)
    twin = me + 1 - 2 * core
    chips = ncol // 2
    side = math.isqrt(chips)
    mx, my = me // (2 * side), lax.rem(me // 2, side)
    every, same = orders(ncol)

    def peer(offset):
        x, y, c = offset
        x, y, c = lax.rem(mx + x, side), lax.rem(my + y, side), lax.rem(core + c, 2)
        return (x * side + y) * 2 + c

    barrier = pltpu.get_barrier_semaphore()

    @pl.loop(1, ncol)
    def _(d):
        pl.semaphore_signal(barrier, inc=1, device_id={"col": lax.rem(me + d, ncol)}, device_id_type=MESH)

    @pl.loop(1, nrow)
    def _(d):
        pl.semaphore_signal(barrier, inc=1, device_id={"row": lax.rem(mz + d, nrow)}, device_id_type=MESH)

    pl.semaphore_wait(barrier, ncol + nrow - 2)

    def send(src, dst, phase, to):
        pltpu.make_async_remote_copy(
            src_ref=src,
            dst_ref=dst,
            send_sem=sems.at[2 * phase],
            recv_sem=sems.at[2 * phase + 1],
            device_id=to,
            device_id_type=MESH,
        ).start()

    def drain(ref, which):
        pltpu.make_async_copy(ref, ref, sems.at[which]).wait()

    def slab(owner):
        return pl.ds(pl.multiple_of(owner * rows, rows), rows)

    def strip_of(owner):
        return pl.ds(pl.multiple_of(owner * strip, strip), strip)

    for offset in every:
        to = peer(offset)
        send(kids_ref.at[:, slab(to), :], got.at[me], 0, {"col": to})

    got[me] = kids_ref[:, slab(me), :]
    drain(got.at[pl.ds(0, ncol - 1)], 1)

    def place(to):
        for child in range(2):
            for half in range(2):
                block = inv_ref[child, 2 * to + half]
                pair = got[block // 2, child]
                low = jnp.broadcast_to(lax.rem(block, 2), (rows, PANEL)) == 0
                out[to, child, :, half * PANEL : (half + 1) * PANEL] = jnp.where(
                    low, pair[:, :PANEL], pair[:, PANEL:]
                )

    place(0)

    for offset in same:
        send(out.at[0], panel_ref.at[:, slab(me), :], 1, {"col": peer(offset)})

    panel_ref[:, slab(me), :] = out[0]

    @pl.loop(1, ncol)
    def _(to):
        place(to)

    for offset in every:
        to = peer(offset)
        send(out.at[to], front_ref.at[:, slab(me), :], 2, {"col": to})

    front_ref[:, slab(me), :] = out[me]
    drain(out.at[pl.ds(0, chips - 1)], 3)

    @pl.loop(0, chips)
    def _(i):
        here = panel_ref.at[:, slab(2 * i + core), :]
        send(here, here, 3, {"col": twin})

    drain(out.at[pl.ds(0, chips)], 7)

    pan = panel_ref[...].reshape(-1, WIDE)
    pan_t = split(pan.T)
    local[...] = product(pan_t, split(pan))

    def tile_at(z):
        t = lax.rem(z, ntile)
        top = me * strip + (t // 4) * 8
        return pl.ds(pl.multiple_of(top, 8), 8), pl.ds(pl.multiple_of(lax.rem(t, 4) * 128, 128), 128)

    @pl.loop(1, nrow)
    def _(d):
        to = lax.rem(mz + d, nrow)
        r, c = tile_at(to)
        send(local.at[r, c], tiles.at[mz], 4, {"row": to})

    r, c = tile_at(mz)
    tiles[mz] = local[r, c]
    drain(tiles.at[pl.ds(0, nrow - 1)], 9)
    total = tiles[0]
    for z in range(1, nrow):
        total = total + tiles[z]
    gram[r, c] = total
    for d in range(-(ntile // 2), ntile // 2):
        if d:
            send(gram.at[r, c], gram.at[r, c], 5, {"row": lax.rem(mz + d + nrow, nrow)})

    half = nrow // 2
    last = half // 2 - 1

    def at(offset):
        return lax.rem(mz + offset + 2 * nrow, nrow)

    def copy(src, dst, index, u, hops):
        return pltpu.make_async_remote_copy(
            src_ref=src, dst_ref=dst, send_sem=ring.at[0, index, u], recv_sem=ring.at[1, index, u],
            device_id={"row": at(hops)}, device_id_type=MESH,
        )

    def pairs_down(k, u):
        return copy(part.at[at(2 * k - half), u], pair_down.at[k, u], k, u, -1)

    def pairs_up(k, u):
        return copy(part.at[at(half - 2 - 2 * k), u], pair_up.at[k, u], 4 + k, u, 1)

    def chain_down(k, u):
        return copy(pair_down.at[k, u], sum_down.at[k, u], 8 + k, u, -2 if k < last else -1)

    def chain_up(k, u):
        src = pair_up.at[k - 1, u] if k else part.at[at(half - 1), u]
        return copy(src, sum_up.at[k, u], 12 + k, u, 2 if k < last else 1)

    def share_up(k, u):
        here = s_ref.at[at(1 - 2 * k if k else 0), u]
        return copy(here, here, 16 + k, u, 2 if k else 1)

    def aside_up(k, u):
        here = s_ref.at[at(-2 * k - 1), u]
        return copy(here, here, 20 + k, u, 1)

    def share_down(k, u):
        here = s_ref.at[at(2 * k - 1 if k else 0), u]
        return copy(here, here, 24 + k, u, -2 if k else -1)

    def aside_down(k, u):
        here = s_ref.at[at(2 * k + 1), u]
        return copy(here, here, 28 + k, u, -1)

    def ring_start(u):
        for k in range(last + 1):
            pairs_down(k, u).start()
            if k == 0:
                chain_up(0, u).start()
            if k < last:
                pairs_up(k, u).start()

    def ring_sum(k, u):
        pairs_down(k, u).wait_recv()
        value = pair_down[k, u] + part[at(2 * k + 1 - half), u]
        if k:
            chain_down(k - 1, u).wait_recv()
            value = value + sum_down[k - 1, u]
        pair_down[k, u] = value
        chain_down(k, u).start()
        if k:
            pairs_up(k - 1, u).wait_recv()
            chain_up(k - 1, u).wait_recv()
            pair_up[k - 1, u] = pair_up[k - 1, u] + part[at(half - 1 - 2 * k), u] + sum_up[k - 1, u]
            chain_up(k, u).start()

    def ring_turn(u):
        chain_down(last, u).wait_recv()
        chain_up(last, u).wait_recv()
        s_ref[mz, u] = part[mz, u] + sum_down[last, u] + sum_up[last, u]
        share_up(0, u).start()
        share_down(0, u).start()

    def ring_share(k, u):
        share_up(k, u).wait_recv()
        if k < last:
            share_up(k + 1, u).start()
        aside_up(k, u).start()
        share_down(k, u).wait_recv()
        if k < last:
            share_down(k + 1, u).start()
            aside_down(k, u).start()

    def ring_end(u):
        for k in range(last + 1):
            aside_up(k, u).wait_recv()
            if k < last:
                aside_down(k, u).wait_recv()

    both = range(2)
    points = [functools.partial(ring_sum, k, u) for k in range(last + 1) for u in both]
    points += [functools.partial(ring_turn, u) for u in both]
    points += [functools.partial(ring_share, k, u) for k in range(last + 1) for u in both]

    drain(out.at[pl.ds(0, ncol - 1)], 5)
    fr = split(front_ref[...].reshape(-1, WIDE))
    for u in both:
        columns = slice(u * PANEL, (u + 1) * PANEL)
        part[:, u] = product(pan_t, (fr[0][:, columns], fr[1][:, columns])).reshape(nrow, chunk, PANEL)
        ring_start(u)

    drain(tiles.at[pl.ds(0, ntile - 1)], 11)
    for offset in same:
        here = gram.at[strip_of(me), :]
        send(here, here, 6, {"col": peer(offset)})
    for _ in range(4):
        points.pop(0)()
    drain(out.at[pl.ds(0, chips - 1)], 13)

    @pl.loop(0, chips)
    def _(i):
        here = gram.at[strip_of(2 * i + core), :]
        send(here, here, 7, {"col": twin})

    drain(out.at[pl.ds(0, chips)], 15)
    drain(out.at[pl.ds(0, chips)], 14)
    drain(out.at[pl.ds(0, chips - 1)], 12)
    drain(tiles.at[pl.ds(0, ntile - 1)], 10)
    linv_ref[...] = jnp.zeros((WIDE, WIDE), F32)
    row_id = lax.broadcasted_iota(jnp.int32, (128, 128), 0)
    col_id = lax.broadcasted_iota(jnp.int32, (128, 128), 1)
    eye = jnp.where(row_id == col_id, 1.0, 0.0)
    for ob in range(WIDE // 128):
        lo, hi = 128 * ob, 128 * (ob + 1)
        diag[...] = gram[lo:hi, lo:hi]
        dinv[...] = eye
        for quarter in range(4):
            count = 32 // DEEP

            @pl.loop(0, count)
            def _(i):
                eliminate(diag, dinv, count * quarter + i)

            if points:
                points.pop(0)()
        lower = jnp.where(row_id >= col_id, dinv[...], 0.0)
        inv = split(lower)
        linv_ref[lo:hi, lo:hi] = lower
        if ob:
            linv_ref[lo:hi, :lo] = product(inv, split(linv_ref[lo:hi, :lo]))
        if hi < WIDE:
            right = product(inv, split(gram[lo:hi, hi:]))
            right_t = split(right.T)
            gram[hi:, hi:] = gram[hi:, hi:] - product(right_t, split(right))
            linv_ref[hi:, :hi] = linv_ref[hi:, :hi] - product(right_t, split(linv_ref[lo:hi, :hi]))
    while points:
        points.pop(0)()
    for u in both:
        ring_end(u)
    for u in both:
        for k in range(last + 1):
            for move in (pairs_down, chain_down, chain_up, share_up, aside_up, share_down):
                move(k, u).wait_send()
            if k < last:
                pairs_up(k, u).wait_send()
                aside_down(k, u).wait_send()
    drain(tiles.at[pl.ds(0, nrow - 1)], 8)
    drain(out.at[pl.ds(0, chips)], 6)
    drain(out.at[pl.ds(0, ncol - 1)], 4)
    drain(out.at[pl.ds(0, chips - 1)], 2)
    drain(out.at[pl.ds(0, ncol - 1)], 0)


def merged(children, inverse, nrow, ncol):
    rows_dev = children.shape[1]
    chunk = WIDE // nrow
    quarter = nrow // 4
    piece = jax.ShapeDtypeStruct((2, rows_dev, WIDE), F32)
    slices = pltpu.VMEM((ncol, 2, rows_dev // ncol, WIDE), F32)
    return pl.pallas_call(
        functools.partial(merge_kernel, nrow, ncol),
        out_shape=(
            piece,
            piece,
            jax.ShapeDtypeStruct((nrow, 2, chunk, PANEL), F32),
            jax.ShapeDtypeStruct((WIDE, WIDE), F32),
        ),
        in_specs=[SMEM, VMEM],
        out_specs=(VMEM, VMEM, VMEM, VMEM),
        scratch_shapes=[
            slices,
            slices,
            pltpu.VMEM((WIDE, WIDE), F32),
            pltpu.VMEM((WIDE, WIDE), F32),
            pltpu.VMEM((nrow, 8, 128), F32),
            pltpu.VMEM((nrow, 2, chunk, PANEL), F32),
            pltpu.VMEM((quarter, 2, chunk, PANEL), F32),
            pltpu.VMEM((quarter - 1, 2, chunk, PANEL), F32),
            pltpu.VMEM((quarter, 2, chunk, PANEL), F32),
            pltpu.VMEM((quarter, 2, chunk, PANEL), F32),
            pltpu.VMEM((128, 128), F32),
            pltpu.VMEM((128, 128), F32),
            pltpu.SemaphoreType.DMA((16,)),
            pltpu.SemaphoreType.DMA((2, 32, 2)),
        ],
        compiler_params=pltpu.CompilerParams(
            collective_id=0, has_side_effects=True, vmem_limit_bytes=48 << 20
        ),
        name="merge",
    )(inverse, children)


def finish_kernel(front_ref, panel_ref, s_ref, linv_ref, rows_ref, trail_ref):
    inv = split(linv_ref[...])
    summed = jnp.concatenate([s_ref[:, u].reshape(WIDE, PANEL) for u in range(2)], axis=1)
    upper = product(inv, split(summed))
    rows_ref[...] = upper
    back = product(split(linv_ref[...].T), split(upper))
    pan = panel_ref[...].reshape(-1, WIDE)
    trail_ref[...] = front_ref[...] - product(split(pan), split(back)).reshape(front_ref.shape)


def finish(front, panel, s, linv):
    return pl.pallas_call(
        finish_kernel,
        out_shape=(
            jax.ShapeDtypeStruct((WIDE, WIDE), F32),
            jax.ShapeDtypeStruct(front.shape, F32),
        ),
        in_specs=[VMEM] * 4,
        out_specs=(VMEM, VMEM),
        compiler_params=pltpu.CompilerParams(vmem_limit_bytes=48 << 20),
        name="finish",
    )(front, panel, s, linv)


def inverted(maps):
    count = maps.shape[1]
    ids = lax.broadcasted_iota(jnp.int32, (2, count, count), 1)
    hit = maps[:, :, None] == lax.broadcasted_iota(jnp.int32, (2, count, count), 2)
    return jnp.sum(jnp.where(hit, ids, 0), axis=1)


def per_device(children, block_maps):
    ncol = lax.axis_size("col")
    nrow = lax.axis_size("row")
    front, panel, s, linv = merged(children, inverted(block_maps), nrow, ncol)
    return finish(front, panel, s, linv)


def solution(mesh):
    placed = (P(None, "row", "col"), P())
    return jax.shard_map(
        per_device,
        mesh=mesh,
        in_specs=placed,
        out_specs=(P(None, "col"), P(None, "row", "col")),
        check_vma=False,
    )
```

```python
import functools
import math

import jax
import jax.numpy as jnp
from jax import lax
from jax.experimental import pallas as pl
from jax.experimental.pallas import tpu as pltpu
from jax.sharding import PartitionSpec as P

PANEL = 256
WIDE = 2 * PANEL
F32 = jnp.float32
BF16 = jnp.bfloat16
MESH = pl.DeviceIdType.MESH
VMEM = pl.BlockSpec(memory_space=pltpu.VMEM)
SMEM = pl.BlockSpec(memory_space=pltpu.SMEM)


def split(x):
    high = x.astype(BF16)
    low = (x - high.astype(F32)).astype(BF16)
    return high, low


def product(a, b, dims=((1,), (0,))):
    def one(x, y):
        return lax.dot_general(x, y, (dims, ((), ())), preferred_element_type=F32)

    return one(a[0], b[0]) + (one(a[0], b[1]) + one(a[1], b[0]))


DEEP = 16


def eliminate(gram, linv, k):
    groups = DEEP // 8
    top = pl.multiple_of(DEEP * k, DEEP)
    rows = [gram[pl.ds(top + 8 * g, 8), :] for g in range(groups)]
    invs = [linv[pl.ds(top + 8 * g, 8), :] for g in range(groups)]
    cols = []
    for g in range(groups):
        turned = pltpu.roll(rows[g], lax.rem(128 - DEEP * k, 128), axis=1)
        cols.append([jnp.broadcast_to(turned[:, j : j + 1], (8, 128)) for j in range(DEEP)])
    sub = lax.broadcasted_iota(jnp.int32, (8, 128), 0)

    def spread(value, i):
        return jnp.broadcast_to(value[i : i + 1, :], (8, 128))

    for p in range(DEEP):
        home, i = divmod(p, 8)
        pivot = spread(cols[home][p], i)
        recip = 1.0 / pivot
        mult = {}
        for g in range(home, groups):
            mult[g] = cols[g][p] * recip
        mult[home] = jnp.where(sub > i, mult[home], 0.0)
        for j in range(p + 1, DEEP):
            across = spread(cols[j // 8][p], j % 8)
            for g in range(j // 8, groups):
                cols[g][j] = cols[g][j] - mult[g] * across
        row, inv = spread(rows[home], i), spread(invs[home], i)
        for g in range(home, groups):
            rows[g] = rows[g] - mult[g] * row
            invs[g] = invs[g] - mult[g] * inv
        scale = jnp.where(sub == i, lax.rsqrt(pivot), 1.0)
        rows[home] = rows[home] * scale
        invs[home] = invs[home] * scale
    both = jnp.concatenate([jnp.concatenate(rows, axis=0), jnp.concatenate(invs, axis=0)], axis=1)
    gram[pl.ds(top, DEEP), :] = both[:, :128]
    linv[pl.ds(top, DEEP), :] = both[:, 128:]
    high, low = split(both)
    left = jnp.concatenate([high[:, :128], low[:, :128], high[:, :128]], axis=0)
    update = lax.dot_general(
        left,
        jnp.concatenate([high, high, low], axis=0),
        (((0,), (0,)), ((), ())),
        preferred_element_type=F32,
    )
    below = lax.broadcasted_iota(jnp.int32, (128, 128), 0) >= top + DEEP
    gram[...] = gram[...] - jnp.where(below, update[:, :128], 0.0)
    linv[...] = linv[...] - jnp.where(below, update[:, 128:], 0.0)


def orders(ncol):
    side = math.isqrt(ncol // 2)
    span = [(x, y, c) for x in range(side) for y in range(side) for c in range(2)]

    def far(o):
        return min(o[0], side - o[0]) + min(o[1], side - o[1])

    every = sorted(span[1:], key=lambda o: -far(o))
    return every, [o for o in every if o[2] == 0]


def merge_kernel(
    nrow, ncol, inv_ref, kids_ref, front_ref, basis_ref, s_ref, linv_ref,
    panel_ref, got, out, local, gram, tiles, part, pair_down, pair_up, sum_down, sum_up, diag, dinv, sems, ring, known
):
    me = lax.axis_index("col")
    mz = lax.axis_index("row")
    rows = kids_ref.shape[1] // ncol
    strip = WIDE // ncol
    chunk = WIDE // nrow
    ntile = strip // 8 * (WIDE // 128)
    core = lax.rem(me, 2)
    twin = me + 1 - 2 * core
    chips = ncol // 2
    side = math.isqrt(chips)
    mx, my = me // (2 * side), lax.rem(me // 2, side)
    every, same = orders(ncol)

    def peer(offset):
        x, y, c = offset
        x, y, c = lax.rem(mx + x, side), lax.rem(my + y, side), lax.rem(core + c, 2)
        return (x * side + y) * 2 + c

    barrier = pltpu.get_barrier_semaphore()

    @pl.loop(1, ncol)
    def _(d):
        pl.semaphore_signal(barrier, inc=1, device_id={"col": lax.rem(me + d, ncol)}, device_id_type=MESH)

    def greet(semaphore, hops):
        for d in (hops, nrow - hops):
            pl.semaphore_signal(
                semaphore, inc=1, device_id={"row": lax.rem(mz + d, nrow)}, device_id_type=MESH
            )

    greet(barrier, 1)
    pl.semaphore_wait(barrier, ncol + 1)

    def send(src, dst, phase, to):
        pltpu.make_async_remote_copy(
            src_ref=src,
            dst_ref=dst,
            send_sem=sems.at[2 * phase],
            recv_sem=sems.at[2 * phase + 1],
            device_id=to,
            device_id_type=MESH,
        ).start()

    def drain(ref, which):
        pltpu.make_async_copy(ref, ref, sems.at[which]).wait()

    def slab(owner):
        return pl.ds(pl.multiple_of(owner * rows, rows), rows)

    def strip_of(owner):
        return pl.ds(pl.multiple_of(owner * strip, strip), strip)

    for offset in every:
        to = peer(offset)
        send(kids_ref.at[:, slab(to), :], got.at[me], 0, {"col": to})

    got[me] = kids_ref[:, slab(me), :]
    hops = 1
    for level in range(3):
        greet(known.at[level], hops)
        pl.semaphore_wait(known.at[level], 2)
        hops *= 2
    drain(got.at[pl.ds(0, ncol - 1)], 1)

    def place(to):
        for child in range(2):
            for half in range(2):
                block = inv_ref[child, 2 * to + half]
                pair = got[block // 2, child]
                low = jnp.broadcast_to(lax.rem(block, 2), (rows, PANEL)) == 0
                out[to, half, child] = jnp.where(low, pair[:, :PANEL], pair[:, PANEL:])

    place(0)

    for offset in same:
        send(out.at[0], panel_ref.at[:, :, slab(me), :], 1, {"col": peer(offset)})

    panel_ref[:, :, slab(me), :] = out[0]

    @pl.loop(1, ncol)
    def _(to):
        place(to)

    for half in range(2):
        columns = slice(half * PANEL, (half + 1) * PANEL)
        for offset in every:
            to = peer(offset)
            send(out.at[to, half], front_ref.at[:, slab(me), columns], (2, 8)[half], {"col": to})
        front_ref[:, slab(me), columns] = out[me, half]

    drain(out.at[pl.ds(0, chips - 1)], 3)

    @pl.loop(0, chips)
    def _(i):
        here = panel_ref.at[:, :, slab(2 * i + core), :]
        send(here, here, 3, {"col": twin})

    drain(out.at[pl.ds(0, chips)], 7)

    pan = jnp.concatenate([panel_ref[u].reshape(-1, PANEL) for u in range(2)], axis=1)
    pan_t = split(pan.T)
    local[...] = product(pan_t, split(pan))

    def tile_at(z):
        t = lax.rem(z, ntile)
        top = me * strip + (t // 4) * 8
        return pl.ds(pl.multiple_of(top, 8), 8), pl.ds(pl.multiple_of(lax.rem(t, 4) * 128, 128), 128)

    @pl.loop(1, nrow)
    def _(d):
        to = lax.rem(mz + d, nrow)
        r, c = tile_at(to)
        send(local.at[r, c], tiles.at[mz], 4, {"row": to})

    r, c = tile_at(mz)
    tiles[mz] = local[r, c]
    half = nrow // 2
    last = half // 2 - 1

    def at(offset):
        return lax.rem(mz + offset + 2 * nrow, nrow)

    def copy(src, dst, index, u, hops):
        return pltpu.make_async_remote_copy(
            src_ref=src, dst_ref=dst, send_sem=ring.at[0, index, u], recv_sem=ring.at[1, index, u],
            device_id={"row": at(hops)}, device_id_type=MESH,
        )

    def pairs_down(k, u):
        return copy(part.at[at(2 * k - half), u], pair_down.at[k, u], k, u, -1)

    def pairs_up(k, u):
        return copy(part.at[at(half - 2 - 2 * k), u], pair_up.at[k, u], 4 + k, u, 1)

    def chain_down(k, u):
        return copy(pair_down.at[k, u], sum_down.at[k, u], 8 + k, u, -2 if k < last else -1)

    def chain_up(k, u):
        src = pair_up.at[k - 1, u] if k else part.at[at(half - 1), u]
        return copy(src, sum_up.at[k, u], 12 + k, u, 2 if k < last else 1)

    def share_up(k, u):
        here = s_ref.at[at(1 - 2 * k if k else 0), u]
        return copy(here, here, 16 + k, u, 2 if k else 1)

    def aside_up(k, u):
        here = s_ref.at[at(-2 * k - 1), u]
        return copy(here, here, 20 + k, u, 1)

    def share_down(k, u):
        here = s_ref.at[at(2 * k - 1 if k else 0), u]
        return copy(here, here, 24 + k, u, -2 if k else -1)

    def aside_down(k, u):
        here = s_ref.at[at(2 * k + 1), u]
        return copy(here, here, 28 + k, u, -1)

    def ring_start(k, u):
        pairs_down(k, u).start()
        if k == 0:
            chain_up(0, u).start()
        if k < last:
            pairs_up(k, u).start()

    def ring_sum(k, u):
        pairs_down(k, u).wait_recv()
        value = pair_down[k, u] + part[at(2 * k + 1 - half), u]
        if k:
            chain_down(k - 1, u).wait_recv()
            value = value + sum_down[k - 1, u]
        pair_down[k, u] = value
        chain_down(k, u).start()
        if k:
            pairs_up(k - 1, u).wait_recv()
            chain_up(k - 1, u).wait_recv()
            pair_up[k - 1, u] = pair_up[k - 1, u] + part[at(half - 1 - 2 * k), u] + sum_up[k - 1, u]
            chain_up(k, u).start()

    def ring_turn(u):
        chain_down(last, u).wait_recv()
        chain_up(last, u).wait_recv()
        s_ref[mz, u] = part[mz, u] + sum_down[last, u] + sum_up[last, u]
        share_up(0, u).start()
        share_down(0, u).start()

    def ring_share(k, u):
        share_up(k, u).wait_recv()
        if k < last:
            share_up(k + 1, u).start()
        aside_up(k, u).start()
        share_down(k, u).wait_recv()
        if k < last:
            share_down(k + 1, u).start()
            aside_down(k, u).start()

    def ring_end(u):
        for k in range(last + 1):
            aside_up(k, u).wait_recv()
            if k < last:
                aside_down(k, u).wait_recv()

    both = range(2)
    points = [functools.partial(ring_sum, k, u) for k in range(last + 1) for u in both]
    points += [functools.partial(ring_turn, u) for u in both]
    points += [functools.partial(ring_share, k, u) for k in range(last + 1) for u in both]

    for u in both:
        columns = slice(u * PANEL, (u + 1) * PANEL)
        drain(out.at[pl.ds(0, ncol - 1), 0], (5, 17)[u])
        fr = split(front_ref[:, :, columns].reshape(-1, PANEL))
        part[:, u] = product(pan_t, fr).reshape(nrow, chunk, PANEL)
        ring_start(0, u)

    drain(tiles.at[pl.ds(0, nrow - 1)], 9)
    total = tiles[0]
    for z in range(1, nrow):
        total = total + tiles[z]
    gram[r, c] = total
    for d in range(-(ntile // 2), ntile // 2):
        if d:
            send(gram.at[r, c], gram.at[r, c], 5, {"row": lax.rem(mz + d + nrow, nrow)})
    for k in range(1, last + 1):
        for u in both:
            ring_start(k, u)
    drain(tiles.at[pl.ds(0, ntile - 1)], 11)
    for offset in same:
        here = gram.at[strip_of(me), :]
        send(here, here, 6, {"col": peer(offset)})
    for _ in range(6):
        points.pop(0)()
    drain(out.at[pl.ds(0, chips - 1)], 13)

    @pl.loop(0, chips)
    def _(i):
        here = gram.at[strip_of(2 * i + core), :]
        send(here, here, 7, {"col": twin})

    drain(out.at[pl.ds(0, chips)], 15)
    drain(out.at[pl.ds(0, chips)], 14)
    drain(out.at[pl.ds(0, chips - 1)], 12)
    drain(tiles.at[pl.ds(0, ntile - 1)], 10)
    linv_ref[...] = jnp.zeros((WIDE, WIDE), F32)
    row_id = lax.broadcasted_iota(jnp.int32, (128, 128), 0)
    col_id = lax.broadcasted_iota(jnp.int32, (128, 128), 1)
    eye = jnp.where(row_id == col_id, 1.0, 0.0)
    for ob in range(WIDE // 128):
        lo, hi = 128 * ob, 128 * (ob + 1)
        diag[...] = gram[lo:hi, lo:hi]
        dinv[...] = eye
        for quarter in range(4):
            count = 32 // DEEP

            @pl.loop(0, count)
            def _(i):
                eliminate(diag, dinv, count * quarter + i)

            if points:
                points.pop(0)()
        lower = jnp.where(row_id >= col_id, dinv[...], 0.0)
        inv = split(lower)
        linv_ref[lo:hi, lo:hi] = lower
        if ob:
            linv_ref[lo:hi, :lo] = product(inv, split(linv_ref[lo:hi, :lo]))
        if hi < WIDE:
            right = product(inv, split(gram[lo:hi, hi:]))
            right_t = split(right.T)
            gram[hi:, hi:] = gram[hi:, hi:] - product(right_t, split(right))
            linv_ref[hi:, :hi] = linv_ref[hi:, :hi] - product(right_t, split(linv_ref[lo:hi, :hi]))
    if points:
        points.pop(0)()
    factor_t = split(linv_ref[...].T)
    pan = jnp.concatenate([panel_ref[u].reshape(-1, PANEL) for u in range(2)], axis=1)
    basis_ref[...] = product(split(pan), factor_t).reshape(basis_ref.shape)
    while points:
        points.pop(0)()
    for u in both:
        ring_end(u)
    for u in both:
        for k in range(last + 1):
            for move in (pairs_down, chain_down, chain_up, share_up, aside_up, share_down):
                move(k, u).wait_send()
            if k < last:
                pairs_up(k, u).wait_send()
                aside_down(k, u).wait_send()
    drain(tiles.at[pl.ds(0, nrow - 1)], 8)
    drain(out.at[pl.ds(0, chips)], 6)
    drain(out.at[pl.ds(0, ncol - 1), 0], 4)
    drain(out.at[pl.ds(0, ncol - 1), 1], 16)
    drain(out.at[pl.ds(0, chips - 1)], 2)
    drain(out.at[pl.ds(0, ncol - 1)], 0)


def merged(children, inverse, nrow, ncol):
    rows_dev = children.shape[1]
    chunk = WIDE // nrow
    quarter = nrow // 4
    piece = jax.ShapeDtypeStruct((2, rows_dev, WIDE), F32)
    return pl.pallas_call(
        functools.partial(merge_kernel, nrow, ncol),
        out_shape=(
            piece,
            piece,
            jax.ShapeDtypeStruct((nrow, 2, chunk, PANEL), F32),
            jax.ShapeDtypeStruct((WIDE, WIDE), F32),
        ),
        in_specs=[SMEM, VMEM],
        out_specs=(VMEM, VMEM, VMEM, VMEM),
        scratch_shapes=[
            pltpu.VMEM((2, 2, rows_dev, PANEL), F32),
            pltpu.VMEM((ncol, 2, rows_dev // ncol, WIDE), F32),
            pltpu.VMEM((ncol, 2, 2, rows_dev // ncol, PANEL), F32),
            pltpu.VMEM((WIDE, WIDE), F32),
            pltpu.VMEM((WIDE, WIDE), F32),
            pltpu.VMEM((nrow, 8, 128), F32),
            pltpu.VMEM((nrow, 2, chunk, PANEL), F32),
            pltpu.VMEM((quarter, 2, chunk, PANEL), F32),
            pltpu.VMEM((quarter - 1, 2, chunk, PANEL), F32),
            pltpu.VMEM((quarter, 2, chunk, PANEL), F32),
            pltpu.VMEM((quarter, 2, chunk, PANEL), F32),
            pltpu.VMEM((128, 128), F32),
            pltpu.VMEM((128, 128), F32),
            pltpu.SemaphoreType.DMA((18,)),
            pltpu.SemaphoreType.DMA((2, 32, 2)),
            pltpu.SemaphoreType.REGULAR((3,)),
        ],
        compiler_params=pltpu.CompilerParams(
            collective_id=0, has_side_effects=True, vmem_limit_bytes=48 << 20
        ),
        name="merge",
    )(inverse, children)


def finish_kernel(front_ref, basis_ref, s_ref, linv_ref, rows_ref, trail_ref):
    summed = jnp.concatenate([s_ref[:, u].reshape(WIDE, PANEL) for u in range(2)], axis=1)
    upper = product(split(linv_ref[...]), split(summed))
    rows_ref[...] = upper
    basis = split(basis_ref[...].reshape(-1, WIDE))
    trail_ref[...] = front_ref[...] - product(basis, split(upper)).reshape(front_ref.shape)


def finish(front, basis, s, linv):
    return pl.pallas_call(
        finish_kernel,
        out_shape=(
            jax.ShapeDtypeStruct((WIDE, WIDE), F32),
            jax.ShapeDtypeStruct(front.shape, F32),
        ),
        in_specs=[VMEM] * 4,
        out_specs=(VMEM, VMEM),
        compiler_params=pltpu.CompilerParams(vmem_limit_bytes=48 << 20),
        name="finish",
    )(front, basis, s, linv)


def inverted(maps):
    count = maps.shape[1]
    ids = lax.broadcasted_iota(jnp.int32, (2, count, count), 1)
    hit = maps[:, :, None] == lax.broadcasted_iota(jnp.int32, (2, count, count), 2)
    return jnp.sum(jnp.where(hit, ids, 0), axis=1)


def per_device(children, block_maps):
    ncol = lax.axis_size("col")
    nrow = lax.axis_size("row")
    front, basis, s, linv = merged(children, inverted(block_maps), nrow, ncol)
    return finish(front, basis, s, linv)


def solution(mesh):
    placed = (P(None, "row", "col"), P())
    return jax.shard_map(
        per_device,
        mesh=mesh,
        in_specs=placed,
        out_specs=(P(None, "col"), P(None, "row", "col")),
        check_vma=False,
    )
```
